512 devices in a mesh: row: 16 (over y, core), col: 32 (over z, x).
Axes of the slice: x: 4, y: 8, z: 8, core: 2. Of those that a mesh axis runs over, the one named last changes fastest.
Arguments:
- features: bfloat16 [131072, 128], P('col', 'row'), may hold values from -6 to 6
- block_codes: int32 [16, 12288], P('row', 'col'), may hold values from 0 to 8191
- block_count: int32 [16, 32], P('row', 'col'), may hold values from 1 to 384, as said below
- block_values: bfloat16 [16, 12288, 4096], P('row', 'col'), may hold values from -0.119628906 to 0.119628906
- weight: bfloat16 [128, 256], replicated, may hold values from -0.5 to 0.5
- bias: float32 [256], replicated, may hold values from -3 to 3
Outputs:
- activated: bfloat16 [131072, 256], P(('row', 'col'))
The draws below stay inside these ranges and needn't reach their ends.
Inputs may be any that keep to these rules, and one draw needn't show every extreme that they name: `block_count`: every tile's count is at most 384; some tile holds exactly 384 in every draw; counts are skewed, the busiest tile about three times the mean. `block_codes`: A code c names local row block c // 64 and local column block c % 64.
All inputs are finite; a program needn't handle non-finite values.
Results may differ from the reference program's by a relative error of at most 0.0045.
Values may be sent and summed in bfloat16 or wider, within the bound.
A program may use at most 128 MiB of HBM per device.

```python
import jax
import jax.numpy as jnp
from jax import lax

F = 128
H = 256
BLK = 64
MAXB = 384
TILE_RB = 128
TILE_CB = 64
NODES = 131072
N_ROW = 16
N_COL = 32


def draw_block_count(key, part):
    first_key, second_key = jax.random.split(jax.random.fold_in(key, 17))
    base = jax.random.randint(first_key, (N_ROW, N_COL), 1, MAXB + 1)
    skewed = jnp.maximum(base * base // MAXB, 1)
    chosen = jax.random.randint(second_key, (), 0, N_ROW * N_COL)
    flat = skewed.reshape(-1)
    flat = jnp.where(jnp.arange(N_ROW * N_COL) == chosen, MAXB, flat)
    return flat.reshape(N_ROW, N_COL).astype(jnp.int32)


def set_ends(array, key, smallest, top_value):
    longest = array.shape.index(max(array.shape))
    spots = []
    for shift in (0, 1):
        where = [jax.random.randint(jax.random.fold_in(key, axis), (), 0, length) for axis, length in enumerate(array.shape)]
        where[longest] = (where[longest] + shift) % array.shape[longest]
        spots.append(tuple(where))
    return array.at[spots[0]].set(smallest).at[spots[1]].set(top_value)


def steps_of(own_key, dims, shards, low, largest):
    gain = 1.0
    for dim, parts in shards:
        heights = jax.random.uniform(jax.random.fold_in(jax.random.fold_in(own_key, 6), dim), (parts,), jnp.float32, low / len(shards), largest / len(shards))
        gain = gain * jnp.repeat(jnp.exp(heights), dims[dim] // parts).reshape((-1,) + (1,) * (len(dims) - 1 - dim))
    return gain


def gaussian(rng, extent, deviation, most, shards=(), held_as=jnp.bfloat16):
    result = jax.random.normal(rng, extent, jnp.float32) * deviation
    if len(shards) > 0:
        result = steps_of(rng, extent, shards, -0.22, 0.18) * result
    return jnp.clip(result, min=-most, max=most).astype(held_as)


def setup_inputs(seed: int = 0) -> dict:
    key_list = jax.random.split(jax.random.key(seed), 7)
    return {
        "features": gaussian(key_list[0], (NODES, F), 1.0, 6.0, ((0, 32), (1, 16))),
        "block_codes": set_ends(jax.random.randint(key_list[1], (N_ROW, N_COL * MAXB), 0, TILE_RB * TILE_CB), jax.random.fold_in(key_list[1], 1), 0, (TILE_RB * TILE_CB) - 1).astype(jnp.int32),
        "block_count": draw_block_count(jax.random.fold_in(key_list[6], 71), 0),
        "block_values": gaussian(key_list[3], (N_ROW, N_COL * MAXB, BLK * BLK), 0.02, 0.119628906, ((0, 16), (1, 32))),
        "weight": gaussian(key_list[4], (F, H), F ** -0.5, 0.5),
        "bias": gaussian(key_list[5], (H,), 0.5, 3.0, (), jnp.float32),
    }


def tile_partial(tile_codes, tile_count, tile_values, column_slab):
    row_block = tile_codes // TILE_CB
    col_block = tile_codes % TILE_CB
    is_live = jnp.arange(MAXB, dtype=jnp.int32) < tile_count
    picked = column_slab[col_block].astype(jnp.float32)
    blocks = tile_values.reshape(MAXB, BLK, BLK).astype(jnp.float32)
    products = jnp.einsum("bij,bjf->bif", blocks, picked)
    products = jnp.where(is_live[:, None, None], products, jnp.zeros_like(products))
    return jax.ops.segment_sum(products, row_block, num_segments=TILE_RB)


def reference(features, block_codes, block_count, block_values, weight, bias):
    slabs = features.reshape(N_COL, TILE_CB, BLK, F)

    def grid_row(index_row):
        row_codes = block_codes[index_row]
        row_values = block_values[index_row]
        row_counts = block_count[index_row]

        def add_tile(total, index_col):
            first_slot = (index_col * MAXB).astype(jnp.int32)
            tile_codes = lax.dynamic_slice_in_dim(row_codes, first_slot, MAXB)
            tile_values = lax.dynamic_slice_in_dim(row_values, first_slot, MAXB, 0)
            return total + tile_partial(tile_codes, row_counts[index_col], tile_values, slabs[index_col]), None

        total, _ = lax.scan(add_tile, jnp.zeros((TILE_RB, BLK, F), jnp.float32), jnp.arange(N_COL, dtype=jnp.int32))
        return total

    sums = lax.map(grid_row, jnp.arange(N_ROW, dtype=jnp.int32))
    aggregated = sums.reshape(NODES, F).astype(jnp.bfloat16)
    hidden = jnp.dot(aggregated, weight, preferred_element_type=jnp.float32) + bias
    return jnp.maximum(hidden, 0.0).astype(jnp.bfloat16)
```

```python
import functools

import jax
import jax.numpy as jnp
from jax import lax
from jax.experimental import pallas as pl
from jax.experimental.pallas import tpu as pltpu
from jax.sharding import PartitionSpec as P

BLK = 64
HALF = BLK // 2
LANES = 128
NX, NZ, NY = 4, 8, 8
UNROLL = 16
MESH = pl.DeviceIdType.MESH
VMEM_LIMIT = 56 << 20


def remote(src, dst, sems, slot, row, col):
    send, recv = sems
    return pltpu.make_async_remote_copy(
        src_ref=src,
        dst_ref=dst,
        send_sem=send.at[slot],
        recv_sem=recv.at[slot],
        device_id=(row, col),
        device_id_type=MESH,
    )


def greet(peers):
    barrier = pltpu.get_barrier_semaphore()
    for peer in peers:
        pl.semaphore_signal(barrier, inc=1, device_id=peer, device_id_type=MESH)
    pl.semaphore_wait(barrier, len(peers))


def gather_kernel(x_ref, slab_ref, send, recv):
    row, col = lax.axis_index("row"), lax.axis_index("col")
    y, core = row // 2, row % 2
    up = lax.rem(y + 1, NY) * 2 + core
    down = lax.rem(y + NY - 1, NY) * 2 + core
    twin = y * 2 + 1 - core
    sems = (send, recv)
    greet([(up, col), (down, col), (twin, col)])
    slab_ref[row] = x_ref[...]
    width = x_ref.shape[1] // 2
    started = []

    def origin(step):
        return lax.rem(y + step + NY, NY) * 2 + core

    def start(ref, slot, to):
        copy = remote(ref, ref, sems, slot, to, col)
        copy.start()
        started.append(copy)
        return copy

    def part(step, half):
        ref = slab_ref.at[origin(step)]
        if half is None:
            return ref
        return ref.at[:, half * width : (half + 1) * width]

    half = NY // 2
    own = part(0, None)
    plus = [start(own, 0, up)]
    minus = [start(own, half, down)]
    twins = [start(own, 2 * half, twin)]
    for step in range(1, half + 1):
        last = step == half
        plus[-1].wait_recv()
        if step < half:
            plus.append(start(part(-step, 0 if step == half - 1 else None), step, up))
        twins.append(start(part(-step, 0 if last else None), 2 * half + 2 * step - 1, twin))
        minus[-1].wait_recv()
        if step < half:
            minus.append(start(part(step, 1 if step == half - 1 else None), half + step, down))
        twins.append(start(part(step, 1 if last else None), 2 * half + 2 * step, twin))
    for copy in twins:
        copy.wait_recv()
    for copy in started:
        copy.wait_send()


def gather(features_t):
    rows, nodes = features_t.shape
    copies = 2 * NY + 1
    return pl.pallas_call(
        gather_kernel,
        out_shape=jax.ShapeDtypeStruct((2 * NY, rows, nodes), features_t.dtype),
        in_specs=[pl.BlockSpec(memory_space=pltpu.VMEM)],
        out_specs=pl.BlockSpec(memory_space=pltpu.VMEM),
        scratch_shapes=[pltpu.SemaphoreType.DMA((copies,)), pltpu.SemaphoreType.DMA((copies,))],
        compiler_params=pltpu.CompilerParams(collective_id=0, has_side_effects=True, vmem_limit_bytes=VMEM_LIMIT),
    )(features_t)


def tile_kernel(codes_ref, count_ref, values_ref, slab_ref, out_ref, flat, blocks, doubled):
    slots = codes_ref.shape[1]
    count = count_ref[0, 0]
    out_ref[...] = jnp.zeros_like(out_ref)

    def relayout(group, _):
        for t in range(HALF):
            rows = values_ref[pl.ds(pl.multiple_of(group * 16, 16), 16), t * LANES : (t + 1) * LANES]
            flat[t * 17 : t * 17 + 16, :] = rows.astype(jnp.float32)
        for s in range(16):
            blocks[group * 16 + s] = flat[pl.ds(s, HALF, stride=17), :].astype(jnp.bfloat16)
        return 0

    groups = (count + UNROLL - 1) // UNROLL
    lax.fori_loop(0, groups, relayout, 0)
    for j in range(slab_ref.shape[1] // LANES):
        nodes = slab_ref[:, j * LANES : (j + 1) * LANES].T
        for h in range(2):
            for copy in range(2):
                doubled[2 * j + h, copy * BLK : (copy + 1) * BLK] = nodes[h * BLK : (h + 1) * BLK]

    lower = lax.broadcasted_iota(jnp.int32, (HALF, LANES), 1) < BLK
    col_blocks = doubled.shape[0]

    def product(slot):
        rows = blocks[slot]
        zero = jnp.zeros_like(rows)
        rows = jnp.where(slot < count, rows, zero)
        left = jnp.concatenate([jnp.where(lower, rows, zero), jnp.where(lower, zero, rows)], 0)
        return jnp.dot(left, doubled[lax.rem(codes_ref[0, slot], col_blocks)], preferred_element_type=jnp.float32)

    def multiply(group, _):
        products = [product(group * UNROLL + u) for u in range(UNROLL)]
        for u in range(UNROLL):
            out_ref[codes_ref[0, group * UNROLL + u] // col_blocks] += products[u]
        return 0

    lax.fori_loop(0, groups, multiply, 0)


def tile(codes, count, values, slab, row_blocks):
    slots = codes.shape[1]
    width, nodes = slab.shape
    return pl.pallas_call(
        tile_kernel,
        out_shape=jax.ShapeDtypeStruct((row_blocks, BLK, width), jnp.float32),
        in_specs=[pl.BlockSpec(memory_space=pltpu.SMEM)] * 2 + [pl.BlockSpec(memory_space=pltpu.VMEM)] * 2,
        out_specs=pl.BlockSpec(memory_space=pltpu.VMEM),
        scratch_shapes=[
            pltpu.VMEM((HALF * 17, LANES), jnp.float32),
            pltpu.VMEM((slots, HALF, LANES), jnp.bfloat16),
            pltpu.VMEM((nodes // BLK, 2 * BLK, width), jnp.bfloat16),
        ],
        compiler_params=pltpu.CompilerParams(vmem_limit_bytes=VMEM_LIMIT),
    )(codes, count, values, slab)


def reduce_kernel(
    part_ref, weight_ref, bias_ref, out_ref,
    zp_out, zp_in, zm_out, zm_in, xs_out, xs_in, xp_out, xp_in, xm_out, xm_in, zs_out, zs_in,
    first, second, total, hidden, send, recv,
):
    row, col = lax.axis_index("row"), lax.axis_index("col")
    z, x = col // NX, col % NX
    sems = (send, recv)
    f32, b16 = jnp.float32, jnp.bfloat16

    def at(dz, dx):
        return lax.rem(z + dz + NZ, NZ) * NX + lax.rem(x + dx + NX, NX)

    def zof(dz):
        return lax.rem(z + dz + NZ, NZ)

    def xof(dx):
        return lax.rem(x + dx + NX, NX)

    greet([(row, at(dz, 0)) for dz in range(1, NZ)] + [(row, at(0, dx)) for dx in range(1, NX)])
    started = []
    slots = iter(range(64))

    def start(src, dst, to):
        copy = remote(src, dst, sems, next(slots), row, to)
        copy.start()
        started.append(copy)
        return copy

    def own(zz, xx, rb):
        return part_ref[zz * NX + xx, rb]

    for xx in range(NX):
        zp_out[0, 0, xx] = own(zof(4), xx, 0).astype(b16)
    zp = [start(zp_out.at[0, 0], zp_in.at[0, 0], at(1, 0))]
    for xx in range(NX):
        zm_out[0, 1, xx] = own(zof(4), xx, 1).astype(b16)
    zm = [start(zm_out.at[0, 1], zm_in.at[0, 1], at(-1, 0))]
    for zz in range(NZ):
        xp_out[0, zz] = own(zz, xof(2), 2).astype(b16)
    xp = [start(xp_out.at[0], xp_in.at[0], at(0, 1))]
    for zz in range(NZ):
        xm_out[0, zz] = own(zz, xof(2), 3).astype(b16)
    xm = [start(xm_out.at[0], xm_in.at[0], at(0, -1))]
    for zz in range(NZ):
        xp_out[1, zz] = own(zz, xof(1), 3).astype(b16)
    xp.append(start(xp_out.at[1], xp_in.at[1], at(0, 1)))
    for zz in range(NZ):
        xm_out[1, zz] = own(zz, xof(-1), 2).astype(b16)
    xm.append(start(xm_out.at[1], xm_in.at[1], at(0, -1)))

    zp[-1].wait_recv()
    for xx in range(NX):
        zp_out[1, 0, xx] = (own(zof(3), xx, 0) + zp_in[0, 0, xx].astype(f32)).astype(b16)
        zp_out[1, 1, xx] = own(zof(3), xx, 1).astype(b16)
    zp.append(start(zp_out.at[1], zp_in.at[1], at(1, 0)))
    zm[-1].wait_recv()
    for xx in range(NX):
        zm_out[1, 1, xx] = (own(zof(-3), xx, 1) + zm_in[0, 1, xx].astype(f32)).astype(b16)
        zm_out[1, 0, xx] = own(zof(-3), xx, 0).astype(b16)
    zm.append(start(zm_out.at[1], zm_in.at[1], at(-1, 0)))

    xp[0].wait_recv()
    for zz in range(NZ):
        xp_out[2, zz] = (own(zz, xof(1), 2) + xp_in[0, zz].astype(f32)).astype(b16)
    xp.append(start(xp_out.at[2], xp_in.at[2], at(0, 1)))
    xm[0].wait_recv()
    for zz in range(NZ):
        xm_out[2, zz] = (own(zz, xof(-1), 3) + xm_in[0, zz].astype(f32)).astype(b16)
    xm.append(start(xm_out.at[2], xm_in.at[2], at(0, -1)))

    for step in (2, 3):
        zp[-1].wait_recv()
        for xx in range(NX):
            for rb in range(2):
                zp_out[step, rb, xx] = (own(zof(4 - step), xx, rb) + zp_in[step - 1, rb, xx].astype(f32)).astype(b16)
        zp.append(start(zp_out.at[step], zp_in.at[step], at(1, 0)))
        zm[-1].wait_recv()
        for xx in range(NX):
            for rb in range(2):
                zm_out[step, rb, xx] = (own(zof(step - 4), xx, rb) + zm_in[step - 1, rb, xx].astype(f32)).astype(b16)
        zm.append(start(zm_out.at[step], zm_in.at[step], at(-1, 0)))

    for copy in xp[1:] + xm[1:]:
        copy.wait_recv()
    for zz in range(NZ):
        second[zz, 0] = own(zz, x, 2) + xp_in[2, zz].astype(f32) + xm_in[1, zz].astype(f32)
        second[zz, 1] = own(zz, x, 3) + xm_in[2, zz].astype(f32) + xp_in[1, zz].astype(f32)
    zs = []
    for dz in range(1, NZ):
        zs_out[dz - 1] = second[zof(dz)].astype(b16)
        zs.append(start(zs_out.at[dz - 1], zs_in.at[dz - 1], at(dz, 0)))

    zp[-1].wait_recv()
    zm[-1].wait_recv()
    for xx in range(NX):
        for rb in range(2):
            first[xx, rb] = own(z, xx, rb) + zp_in[3, rb, xx].astype(f32) + zm_in[3, rb, xx].astype(f32)
    xs = []
    for dx in range(1, NX):
        xs_out[dx - 1] = first[xof(dx)].astype(b16)
        xs.append(start(xs_out.at[dx - 1], xs_in.at[dx - 1], at(0, dx)))

    for copy in zs:
        copy.wait_recv()
    total[2:4] = second[z]
    for dz in range(1, NZ):
        total[2:4] += zs_in[dz - 1].astype(f32)
    for copy in xs:
        copy.wait_recv()
    total[0:2] = first[x]
    for dx in range(1, NX):
        total[0:2] += xs_in[dx - 1].astype(f32)

    for rb in range(4):
        aggregated = total[rb].astype(b16)
        sums = jnp.dot(aggregated, weight_ref[...], preferred_element_type=f32) + bias_ref[...]
        sums = jnp.maximum(sums, 0.0)
        for h in range(2):
            for piece in range(hidden.shape[0]):
                rows = sums[h * HALF : (h + 1) * HALF, piece * LANES : (piece + 1) * LANES]
                hidden[piece, pl.ds(rb * BLK + h, HALF, stride=2), :] = rows
    for piece in range(hidden.shape[0]):
        out_ref[:, piece * LANES : (piece + 1) * LANES] = hidden[piece].astype(b16)
    for copy in started:
        copy.wait_send()


def reduce(part, weight, bias):
    owners, row_blocks, _, width = part.shape
    hid = weight.shape[1]
    b16, f32 = jnp.bfloat16, jnp.float32
    chain = pltpu.VMEM((4, 2, NX, BLK, width), b16)
    across = pltpu.VMEM((3, NZ, BLK, width), b16)
    straight = lambda n: pltpu.VMEM((n - 1, 2, BLK, width), b16)
    copies = 14 + NZ - 1 + NX - 1
    return pl.pallas_call(
        reduce_kernel,
        out_shape=jax.ShapeDtypeStruct((row_blocks * BLK, hid), b16),
        in_specs=[pl.BlockSpec(memory_space=pltpu.VMEM)] * 3,
        out_specs=pl.BlockSpec(memory_space=pltpu.VMEM),
        scratch_shapes=[chain] * 4
        + [straight(NX)] * 2
        + [across] * 4
        + [straight(NZ)] * 2
        + [
            pltpu.VMEM((NX, 2, BLK, width), f32),
            pltpu.VMEM((NZ, 2, BLK, width), f32),
            pltpu.VMEM((4, BLK, width), f32),
            pltpu.VMEM((hid // LANES, 4 * BLK, LANES), f32),
            pltpu.SemaphoreType.DMA((copies,)),
            pltpu.SemaphoreType.DMA((copies,)),
        ],
        compiler_params=pltpu.CompilerParams(collective_id=1, has_side_effects=True, vmem_limit_bytes=VMEM_LIMIT),
    )(part, weight, bias)


def shards(features, block_codes, block_count, block_values, weight, bias):
    slab = gather(features.T)
    slab = slab.reshape(slab.shape[0] * slab.shape[1], slab.shape[2])
    row_blocks = slab.shape[1] * lax.axis_size("col") // lax.axis_size("row") // BLK
    part = tile(block_codes, block_count, block_values[0], slab, row_blocks)
    owners = lax.axis_size("col")
    part = part.reshape(owners, row_blocks // owners, BLK, slab.shape[0])
    return reduce(part, weight, bias.reshape(1, -1))


def solution(mesh):
    in_specs = (P("col", "row"), P("row", "col"), P("row", "col"), P("row", "col", None), P(), P())
    out_specs = P(("row", "col"), None)
    return jax.shard_map(shards, mesh=mesh, in_specs=in_specs, out_specs=out_specs, check_vma=False)
```

```python
import jax
import jax.numpy as jnp
from jax import lax
from jax.experimental import pallas as pl
from jax.experimental.pallas import tpu as pltpu
from jax.sharding import PartitionSpec as P

BLK = 64
HALF = BLK // 2
LANES = 128
OWNED = 4
NX, NZ, NY = 4, 8, 8
UNROLL = 16
GROUPS = ((4, 3), (-3, 2), (-2, 1), (-1, 0))
ORDER = "F0 F1 N0 S0 F2 N1 S1 E0 F3 N2 S2 E1 N3 S3 E2 E3"
MESH = pl.DeviceIdType.MESH
VMEM_LIMIT = 56 << 20
f32, b16, i32 = jnp.float32, jnp.bfloat16, jnp.int32


class Copies:
    def __init__(self, send, recv):
        self.send, self.recv, self.started = send, recv, []

    def __call__(self, src, dst, to):
        slot = len(self.started)
        copy = pltpu.make_async_remote_copy(
            src_ref=src,
            dst_ref=dst,
            send_sem=self.send.at[slot],
            recv_sem=self.recv.at[slot],
            device_id=to,
            device_id_type=MESH,
        )
        copy.start()
        self.started.append(copy)
        return copy


def kernel(
    codes_ref, rows_ref, count_ref, x_ref, values_hbm, out_ref,
    slab, values, flat, blocks, doubled, spread, index, index_smem, chain,
    far_out, far_in, near_out, near_in, sum_out, sum_in, zs_out, zs_in, total, mixed,
    local, send, recv,
):
    row, col = lax.axis_index("row"), lax.axis_index("col")
    y, core = row // 2, row % 2
    z, x = col // NX, col % NX
    slots = values.shape[0]
    col_blocks = doubled.shape[0]
    count = count_ref[0, 0]
    start = Copies(send, recv)

    def ring(step):
        return lax.rem(y + step + NY, NY) * 2 + core

    def zof(dz):
        return lax.rem(z + dz + NZ, NZ)

    def xof(dx):
        return lax.rem(x + dx + NX, NX)

    def at(dz, dx):
        return (row, zof(dz) * NX + xof(dx))

    twin = (y * 2 + 1 - core, col)
    peers = [(ring(s), col) for s in (1, -1, 2, -2)] + [twin]
    peers += [at(dz, 0) for dz in range(1, NZ)] + [at(0, 1), at(0, -1)]
    barrier = pltpu.get_barrier_semaphore()
    for peer in peers:
        pl.semaphore_signal(barrier, inc=1, device_id=peer, device_id_type=MESH)
    load = pltpu.make_async_copy(values_hbm, values, local.at[0])
    load.start()
    keep = pltpu.make_async_copy(x_ref, slab.at[row], local.at[1])
    keep.start()
    pl.semaphore_wait(barrier, len(peers))

    middle = x_ref.shape[1] // 2

    def chunk(step, half=None):
        ref = slab.at[ring(step)]
        return ref if half is None else ref.at[:, half * middle : (half + 1) * middle]

    def forward(step, half, to):
        ref = chunk(step, half)
        return start(ref, ref, to)

    direct = {s: start(x_ref, slab.at[row], (ring(s), col)) for s in (1, -1, 2, -2)}
    twins = [start(x_ref, slab.at[row], twin)]

    for q in range(slots // LANES):
        lanes = jnp.broadcast_to(rows_ref[:, q * LANES : (q + 1) * LANES] // col_blocks, (LANES, LANES))
        spread[q * LANES : (q + 1) * LANES] = lanes.T
    earlier = lax.broadcasted_iota(i32, (slots, LANES), 0)
    lane = lax.broadcasted_iota(i32, (slots, LANES), 1)
    live = jnp.where(earlier < count, earlier + 1, 0)
    for q in range(slots // LANES):
        same = spread[...] == rows_ref[:, q * LANES : (q + 1) * LANES] // col_blocks
        ahead = earlier < lane + q * LANES
        index[q : q + 1] = jnp.max(jnp.where(same & ahead, live, 0), axis=0, keepdims=True)
    index[3:4] = jnp.max(jnp.where(spread[...] == lane, live, 0), axis=0, keepdims=True)
    fetch = pltpu.make_async_copy(index, index_smem, local.at[2])
    fetch.start()
    chain[0] = jnp.zeros(chain.shape[1:], f32)

    forwarded = {}
    for s in (1, -1):
        direct[s].wait_recv()
        forwarded[s] = forward(-s, None, (ring(2 * s), col))
        twins.append(forward(-s, None, twin))

    def relayout(group, _):
        for t in range(HALF):
            rows = values[pl.ds(pl.multiple_of(group * 16, 16), 16), t * LANES : (t + 1) * LANES]
            flat[t * 17 : t * 17 + 16, :] = rows.astype(f32)
        for s in range(16):
            blocks[group * 16 + s] = flat[pl.ds(s, HALF, stride=17), :].astype(b16)
        return 0

    load.wait()
    groups = slots // 16
    lax.fori_loop(0, groups // 3, relayout, 0)
    for s in (2, -2):
        half = 0 if s > 0 else 1
        direct[s].wait_recv()
        forwarded[s] = forward(-s, half, (ring(s), col))
        twins.append(forward(-s, None, twin))
    lax.fori_loop(groups // 3, groups, relayout, 0)
    for s in (1, -1):
        forwarded[s].wait_recv()
        twins.append(forward(-3 * s, None, twin))
    for s in (2, -2):
        forwarded[s].wait_recv()
        twins.append(forward(4, 0 if s > 0 else 1, twin))
    keep.wait()
    fetch.wait()
    for copy in twins:
        copy.wait_recv()

    for j in range(x_ref.shape[1] // LANES):
        nodes = slab[:, :, j * LANES : (j + 1) * LANES].astype(f32).reshape(LANES, LANES).T.astype(b16)
        for h in range(2):
            for copy in range(2):
                doubled[2 * j + h, copy * BLK : (copy + 1) * BLK] = nodes[h * BLK : (h + 1) * BLK]

    lower = lax.broadcasted_iota(i32, (HALF, LANES), 1) < BLK

    def product(slot):
        rows = blocks[slot]
        zero = jnp.zeros_like(rows)
        left = jnp.concatenate([jnp.where(lower, rows, zero), jnp.where(lower, zero, rows)], 0)
        return jnp.dot(left, doubled[lax.rem(codes_ref[0, slot], col_blocks)], preferred_element_type=f32)

    def multiply(group, _):
        products = [product(group * UNROLL + u) for u in range(UNROLL)]
        for u in range(UNROLL):
            slot = group * UNROLL + u
            chain[slot + 1] = products[u] + chain[index_smem[slot // LANES, lax.rem(slot, LANES)]]
        return 0

    lax.fori_loop(0, slots // UNROLL, multiply, 0)

    def own(zz, xx, rb):
        return chain[index_smem[3, (zz * NX + xx) * OWNED + rb]]

    far, near, sums, straight = {}, {}, {}, []

    def send_far(g):
        for d in range(2):
            for i, dz in enumerate(GROUPS[g]):
                for k in range(2):
                    far_out[g, d, i, k] = own(zof(dz), xof(2), 2 * d + k).astype(b16)
            far[g, d] = start(far_out.at[g, d], far_in.at[g, d], at(0, 1 - 2 * d))

    def send_near(g):
        for d in range(2):
            for i, dz in enumerate(GROUPS[g]):
                for k in range(2):
                    near_out[g, d, i, k] = own(zof(dz), xof(1 - 2 * d), 2 * (1 - d) + k).astype(b16)
            near[g, d] = start(near_out.at[g, d], near_in.at[g, d], at(0, 1 - 2 * d))

    def send_sum(g):
        for d in range(2):
            far[g, d].wait_recv()
            for i, dz in enumerate(GROUPS[g]):
                for k in range(2):
                    mine = own(zof(dz), xof(1 - 2 * d), 2 * d + k)
                    sum_out[g, d, i, k] = (mine + far_in[g, d, i, k].astype(f32)).astype(b16)
            sums[g, d] = start(sum_out.at[g, d], sum_in.at[g, d], at(0, 1 - 2 * d))

    def send_straight(g):
        for d in range(2):
            near[g, d].wait_recv()
            sums[g, d].wait_recv()
        for i, dz in enumerate(GROUPS[g]):
            for d in range(2):
                for k in range(2):
                    arrived = sum_in[g, d, i, k].astype(f32) + near_in[g, 1 - d, i, k].astype(f32)
                    value = own(zof(dz), x, 2 * d + k) + arrived
                    if dz == 0:
                        total[2 * d + k] = value
                    else:
                        zs_out[dz + 3, 2 * d + k] = value.astype(b16)
            if dz != 0:
                straight.append((dz, start(zs_out.at[dz + 3], zs_in.at[dz + 3], at(dz, 0))))

    steps = {"F": send_far, "N": send_near, "S": send_sum, "E": send_straight}
    for step in ORDER.split():
        steps[step[0]](int(step[1]))
    for dz, copy in straight:
        copy.wait_recv()
        for rb in range(OWNED):
            total[rb] += zs_in[dz + 3, rb].astype(f32)

    for rb in range(OWNED):
        for h in range(2):
            mixed[pl.ds(rb * BLK + h, HALF, stride=2), :] = total[rb, h * HALF : (h + 1) * HALF]
    out_ref[...] = mixed[...].astype(b16)
    for copy in start.started:
        copy.wait_send()


def aggregate(codes, count, features_t, values):
    slots = codes.shape[1]
    rows, nodes = features_t.shape
    width = 2 * NY * rows
    vmem = pltpu.VMEM
    crossing = vmem((len(GROUPS), 2, 2, 2, BLK, width), b16)
    straight = vmem((NZ, OWNED, BLK, width), b16)
    copies = 4 + 1 + 4 + 8 + 6 * len(GROUPS) + NZ - 1
    return pl.pallas_call(
        kernel,
        out_shape=jax.ShapeDtypeStruct((OWNED * BLK, width), b16),
        in_specs=[
            pl.BlockSpec(memory_space=pltpu.SMEM),
            pl.BlockSpec(memory_space=pltpu.VMEM),
            pl.BlockSpec(memory_space=pltpu.SMEM),
            pl.BlockSpec(memory_space=pl.ANY),
            pl.BlockSpec(memory_space=pl.ANY),
        ],
        out_specs=pl.BlockSpec(memory_space=pltpu.VMEM),
        scratch_shapes=[
            vmem((2 * NY, rows, nodes), b16),
            vmem((slots, BLK * BLK), b16),
            vmem((HALF * 17, LANES), f32),
            vmem((slots, HALF, LANES), b16),
            vmem((nodes // BLK, 2 * BLK, width), b16),
            vmem((slots, LANES), i32),
            vmem((8, LANES), i32),
            pltpu.SMEM((8, LANES), i32),
            vmem((slots + 1, BLK, width), f32),
        ]
        + [crossing] * 6
        + [straight] * 2
        + [
            vmem((OWNED, BLK, width), f32),
            vmem((OWNED * BLK, width), f32),
            pltpu.SemaphoreType.DMA((3,)),
            pltpu.SemaphoreType.DMA((copies,)),
            pltpu.SemaphoreType.DMA((copies,)),
        ],
        compiler_params=pltpu.CompilerParams(collective_id=0, has_side_effects=True, vmem_limit_bytes=VMEM_LIMIT),
    )(codes, codes, count, features_t, values)


def shards(features, block_codes, block_count, block_values, weight, bias):
    aggregated = aggregate(block_codes, block_count, features.T, block_values[0])
    hidden = jnp.dot(aggregated, weight, preferred_element_type=f32) + bias
    return jnp.maximum(hidden, 0.0).astype(b16)


def solution(mesh):
    in_specs = (P("col", "row"), P("row", "col"), P("row", "col"), P("row", "col", None), P(), P())
    out_specs = P(("row", "col"), None)
    return jax.shard_map(shards, mesh=mesh, in_specs=in_specs, out_specs=out_specs, check_vma=False)
```

```python
import jax
import jax.numpy as jnp
from jax import lax
from jax.experimental import pallas as pl
from jax.experimental.pallas import tpu as pltpu
from jax.sharding import PartitionSpec as P

BLK = 64
HALF = BLK // 2
LANES = 128
OWNED = 4
NX, NZ, NY = 4, 8, 8
UNROLL = 64
GROUPS = ((4, 3), (-3, 2), (-2, 1), (-1, 0))
ORDER = ("A1", "F0", "F1", "N0", "A2", "S0", "F2", "N1", "A3", "S1", "E0", "F3")
ORDER += ("N2", "A4", "S2", "E1", "N3", "S3", "X0", "E2", "E3")
MESH = pl.DeviceIdType.MESH
VMEM_LIMIT = 56 << 20
f32, b16, i32 = jnp.float32, jnp.bfloat16, jnp.int32


class Copies:
    def __init__(self, send, recv):
        self.send, self.recv, self.started = send, recv, []

    def __call__(self, src, dst, to):
        slot = len(self.started)
        copy = pltpu.make_async_remote_copy(
            src_ref=src,
            dst_ref=dst,
            send_sem=self.send.at[slot],
            recv_sem=self.recv.at[slot],
            device_id=to,
            device_id_type=MESH,
        )
        copy.start()
        self.started.append(copy)
        return copy


def kernel(
    codes_ref, rows_ref, count_ref, x_ref, values_hbm, out_ref,
    slab, values, flat, blocks, nodes, spread, index, index_smem, chain,
    ring_out, ring_in, across_out, across_in, far_out, far_in, near_out, near_in, sum_out, sum_in,
    straight_out, straight_in, pass_in, total, mixed,
    local, send, recv,
):
    row, col = lax.axis_index("row"), lax.axis_index("col")
    y, core = row // 2, row % 2
    z, x = col // NX, col % NX
    slots = values.shape[0]
    col_blocks = nodes.shape[0]
    count = count_ref[0, 0]
    start = Copies(send, recv)

    def ring(step):
        return lax.rem(y + step + NY, NY) * 2 + core

    def zof(dz):
        return lax.rem(z + dz + NZ, NZ)

    def xof(dx):
        return lax.rem(x + dx + NX, NX)

    def at(dz, dx):
        return (row, zof(dz) * NX + xof(dx))

    twin = (y * 2 + 1 - core, col)
    peers = [(ring(s), col) for s in (1, -1, 2, -2)] + [twin]
    peers += [at(s, 0) for s in (1, -1, 2, -2, 3, -3)] + [at(0, s) for s in (1, -1, 2)]
    barrier = pltpu.get_barrier_semaphore()
    for peer in peers:
        pl.semaphore_signal(barrier, inc=1, device_id=peer, device_id_type=MESH)
    load = pltpu.make_async_copy(values_hbm, values, local.at[0])
    load.start()
    keep = pltpu.make_async_copy(x_ref, slab.at[row], local.at[1])
    keep.start()
    pl.semaphore_wait(barrier, len(peers))

    middle = x_ref.shape[1] // 2

    def chunk(step, half=None):
        ref = slab.at[ring(step)]
        return ref if half is None else ref.at[:, half * middle : (half + 1) * middle]

    def forward(step, half, to):
        ref = chunk(step, half)
        return start(ref, ref, to)

    direct = {s: start(x_ref, slab.at[row], (ring(s), col)) for s in (2, -2, 1, -1)}
    twins = [start(x_ref, slab.at[row], twin)]

    for q in range(slots // LANES):
        lanes = jnp.broadcast_to(rows_ref[:, q * LANES : (q + 1) * LANES] // col_blocks, (LANES, LANES))
        spread[q * LANES : (q + 1) * LANES] = lanes.T
    earlier = lax.broadcasted_iota(i32, (slots, LANES), 0)
    lane = lax.broadcasted_iota(i32, (slots, LANES), 1)
    live = jnp.where(earlier < count, earlier + 1, 0)
    for q in range(slots // LANES):
        same = spread[...] == rows_ref[:, q * LANES : (q + 1) * LANES] // col_blocks
        ahead = earlier < lane + q * LANES
        index[q : q + 1] = jnp.max(jnp.where(same & ahead, live, 0), axis=0, keepdims=True)
    index[3:4] = jnp.max(jnp.where(spread[...] == lane, live, 0), axis=0, keepdims=True)
    fetch = pltpu.make_async_copy(index, index_smem, local.at[2])
    fetch.start()
    chain[0] = jnp.zeros(chain.shape[1:], f32)

    forwarded = {}
    for s in (1, -1):
        direct[s].wait_recv()
        twins.append(forward(-s, None, twin))

    def relayout(group, _):
        for t in range(HALF):
            rows = values[pl.ds(pl.multiple_of(group * 16, 16), 16), t * LANES : (t + 1) * LANES]
            flat[t * 17 : t * 17 + 16, :] = rows.astype(f32)
        for s in range(16):
            rows = flat[pl.ds(s, HALF, stride=17), :]
            blocks[group * 16 + s, 0:HALF] = rows.astype(b16)
            blocks[group * 16 + s, HALF:BLK] = pltpu.roll(rows, BLK, 1).astype(b16)
        return 0

    load.wait()
    groups = slots // 16
    lax.fori_loop(0, groups // 3, relayout, 0)
    for s in (2, -2):
        half = 0 if s > 0 else 1
        direct[s].wait_recv()
        forwarded[s // 2] = forward(-s, None, (ring(s // 2), col))
        forwarded[s] = forward(-s, half, (ring(s), col))
        twins.append(forward(-s, None, twin))
    lax.fori_loop(groups // 3, groups, relayout, 0)
    for s in (1, -1):
        forwarded[s].wait_recv()
        twins.append(forward(-3 * s, None, twin))
    for s in (2, -2):
        forwarded[s].wait_recv()
        twins.append(forward(4, 0 if s > 0 else 1, twin))
    keep.wait()
    fetch.wait()
    for copy in twins:
        copy.wait_recv()

    for j in range(x_ref.shape[1] // LANES):
        taken = slab[:, :, j * LANES : (j + 1) * LANES].astype(f32).reshape(LANES, LANES).T.astype(b16)
        for h in range(2):
            nodes[2 * j + h] = taken[h * BLK : (h + 1) * BLK]

    def product(slot):
        rows = nodes[lax.rem(codes_ref[0, slot], col_blocks)]
        return jnp.dot(blocks[slot, :, 0:BLK], rows, preferred_element_type=f32)

    def multiply(group, _):
        products = [product(group * UNROLL + u) for u in range(UNROLL)]
        for u in range(UNROLL):
            slot = group * UNROLL + u
            chain[slot + 1] = products[u] + chain[index_smem[slot // LANES, lax.rem(slot, LANES)]]
        return 0

    lax.fori_loop(0, slots // UNROLL, multiply, 0)

    def own(zz, xx, piece):
        block = index_smem[3, (zz * NX + xx) * OWNED + piece // 2]
        return chain[block, (piece % 2) * HALF : (piece % 2 + 1) * HALF]

    def wide(ref):
        return ref[...].astype(f32)

    ring_z, first = {}, {}

    def send_ring(step):
        for d in range(2):
            sign = 1 - 2 * d
            if step > 1:
                ring_z[step - 1, d].wait_recv()
            for xx in range(NX):
                for piece in range(2):
                    mine = own(zof(sign * (5 - step)), xx, piece)
                    if step > 2 or (step == 2 and piece == d):
                        mine = mine + wide(ring_in.at[step - 2, d, piece, xx])
                    if step > 1 or piece == d:
                        ring_out[step - 1, d, piece, xx] = mine.astype(b16)
            src, dst = ring_out.at[step - 1, d], ring_in.at[step - 1, d]
            if step == 1:
                src, dst = src.at[d], dst.at[d]
            ring_z[step, d] = start(src, dst, at(sign, 0))

    def send_across(_):
        for d in range(2):
            ring_z[4, d].wait_recv()
        for dx in (2, 1, -1, 0):
            for piece in range(2):
                value = own(z, xof(dx), piece) + wide(ring_in.at[3, 0, piece, xof(dx)])
                value = value + wide(ring_in.at[3, 1, piece, xof(dx)])
                if dx == 0:
                    total[piece] = value
                else:
                    across_out[dx + 1, piece] = value.astype(b16)
            if dx != 0:
                first[dx] = start(across_out.at[dx + 1], across_in.at[dx + 1], at(0, dx))

    far, near, sums, straight, passed = {}, {}, {}, {}, {}

    def send_far(g):
        for d in range(2):
            for i, dz in enumerate(GROUPS[g]):
                for k in range(3):
                    far_out[g, d, i, k] = own(zof(dz), xof(2), 2 + 3 * d + k).astype(b16)
            far[g, d] = start(far_out.at[g, d], far_in.at[g, d], at(0, 1 - 2 * d))

    def send_near(g):
        for d in range(2):
            for i, dz in enumerate(GROUPS[g]):
                for k in range(3):
                    near_out[g, d, i, k] = own(zof(dz), xof(1 - 2 * d), 5 - 3 * d + k).astype(b16)
            near[g, d] = start(near_out.at[g, d], near_in.at[g, d], at(0, 1 - 2 * d))

    def send_sum(g):
        for d in range(2):
            far[g, d].wait_recv()
            for i, dz in enumerate(GROUPS[g]):
                for k in range(3):
                    mine = own(zof(dz), xof(1 - 2 * d), 2 + 3 * d + k)
                    sum_out[g, d, i, k] = (mine + wide(far_in.at[g, d, i, k])).astype(b16)
            sums[g, d] = start(sum_out.at[g, d], sum_in.at[g, d], at(0, 1 - 2 * d))

    def send_straight(g):
        for d in range(2):
            near[g, d].wait_recv()
            sums[g, d].wait_recv()
        for i, dz in enumerate(GROUPS[g]):
            if abs(dz) == 2:
                passed[dz].wait_recv()
            for d in range(2):
                for k in range(3):
                    value = own(zof(dz), x, 2 + 3 * d + k)
                    value = value + (wide(sum_in.at[g, d, i, k]) + wide(near_in.at[g, 1 - d, i, k]))
                    if dz == 2 - 4 * d:
                        value = value + wide(pass_in.at[d, k])
                    if dz == 0:
                        total[2 + 3 * d + k] = value
                    else:
                        straight_out[dz + 3, d, k] = value.astype(b16)
            if dz == 4:
                for d in range(2):
                    passed[2 - 4 * d] = start(straight_out.at[7, d], pass_in.at[d], at(2 - 4 * d, 0))
            elif dz != 0:
                straight[dz] = start(straight_out.at[dz + 3], straight_in.at[dz + 3], at(dz, 0))

    steps = {"A": send_ring, "X": send_across, "F": send_far, "N": send_near, "S": send_sum, "E": send_straight}
    for step in ORDER:
        steps[step[0]](int(step[1]))
    for dz, copy in straight.items():
        copy.wait_recv()
        for d in range(2):
            for k in range(3):
                total[2 + 3 * d + k] += wide(straight_in.at[dz + 3, d, k])
    for dx, copy in first.items():
        copy.wait_recv()
        for piece in range(2):
            total[piece] += wide(across_in.at[dx + 1, piece])

    for rb in range(OWNED):
        for h in range(2):
            mixed[pl.ds(rb * BLK + h, HALF, stride=2), :] = total[2 * rb + h]
    out_ref[...] = mixed[...].astype(b16)
    for copy in start.started:
        copy.wait_send()


def aggregate(codes, count, features_t, values):
    slots = codes.shape[1]
    rows, nodes = features_t.shape
    width = 2 * NY * rows
    vmem = pltpu.VMEM
    crossing = vmem((len(GROUPS), 2, 2, 3, HALF, width), b16)
    ring = vmem((4, 2, 2, NX, HALF, width), b16)
    across = vmem((NX, 2, HALF, width), b16)
    straight = vmem((NZ, 2, 3, HALF, width), b16)
    copies = 4 + 1 + 4 + 8 + 8 + NX - 1 + 6 * len(GROUPS) + NZ
    return pl.pallas_call(
        kernel,
        out_shape=jax.ShapeDtypeStruct((OWNED * BLK, width), b16),
        in_specs=[
            pl.BlockSpec(memory_space=pltpu.SMEM),
            pl.BlockSpec(memory_space=pltpu.VMEM),
            pl.BlockSpec(memory_space=pltpu.SMEM),
            pl.BlockSpec(memory_space=pl.ANY),
            pl.BlockSpec(memory_space=pl.ANY),
        ],
        out_specs=pl.BlockSpec(memory_space=pltpu.VMEM),
        scratch_shapes=[
            vmem((2 * NY, rows, nodes), b16),
            vmem((slots, BLK * BLK), b16),
            vmem((HALF * 17, LANES), f32),
            vmem((slots, BLK, LANES), b16),
            vmem((nodes // BLK, BLK, width), b16),
            vmem((slots, LANES), i32),
            vmem((8, LANES), i32),
            pltpu.SMEM((8, LANES), i32),
            vmem((slots + 1, BLK, width), f32),
        ]
        + [ring] * 2
        + [across] * 2
        + [crossing] * 6
        + [straight] * 2
        + [
            vmem((2, 3, HALF, width), b16),
            vmem((2 * OWNED, HALF, width), f32),
            vmem((OWNED * BLK, width), f32),
            pltpu.SemaphoreType.DMA((3,)),
            pltpu.SemaphoreType.DMA((copies,)),
            pltpu.SemaphoreType.DMA((copies,)),
        ],
        compiler_params=pltpu.CompilerParams(collective_id=0, has_side_effects=True, vmem_limit_bytes=VMEM_LIMIT),
    )(codes, codes, count, features_t, values)


def shards(features, block_codes, block_count, block_values, weight, bias):
    aggregated = aggregate(block_codes, block_count, features.T, block_values[0])
    hidden = jnp.dot(aggregated, weight, preferred_element_type=f32) + bias
    return jnp.maximum(hidden, 0.0).astype(b16)


def solution(mesh):
    in_specs = (P("col", "row"), P("row", "col"), P("row", "col"), P("row", "col", None), P(), P())
    out_specs = P(("row", "col"), None)
    return jax.shard_map(shards, mesh=mesh, in_specs=in_specs, out_specs=out_specs, check_vma=False)
```

```python
import jax
import jax.numpy as jnp
from jax import lax
from jax.experimental import pallas as pl
from jax.experimental.pallas import tpu as pltpu
from jax.sharding import PartitionSpec as P

BLK = 64
HALF = BLK // 2
LANES = 128
OWNED = 4
NX, NZ, NY = 4, 8, 8
UNROLL = 64
GROUPS = ((4,), (3, -3), (2, -2), (1, -1), (0,))
ORDER = ("F0", "F1", "A1", "F2", "F3", "F4", "S0", "N0", "S1", "A2", "N1", "E0", "S2", "N2")
ORDER += ("E1", "S3", "N3", "X0", "E2", "S4", "N4", "E3", "E4")
MESH = pl.DeviceIdType.MESH
VMEM_LIMIT = 56 << 20
f32, b16, i32 = jnp.float32, jnp.bfloat16, jnp.int32


class Copies:
    def __init__(self, send, recv):
        self.send, self.recv, self.started = send, recv, []

    def __call__(self, src, dst, to):
        slot = len(self.started)
        copy = pltpu.make_async_remote_copy(
            src_ref=src,
            dst_ref=dst,
            send_sem=self.send.at[slot],
            recv_sem=self.recv.at[slot],
            device_id=to,
            device_id_type=MESH,
        )
        copy.start()
        self.started.append(copy)
        return copy


def kernel(
    codes_ref, rows_ref, count_ref, x_ref, values_hbm, out_ref,
    slab, values, flat, blocks, nodes, spread, index, index_smem, chain,
    ring_out, ring_in, across_out, across_in, far_out, far_in, near_out, near_in, sum_out, sum_in,
    straight_out, straight_in, total, mixed,
    local, send, recv,
):
    row, col = lax.axis_index("row"), lax.axis_index("col")
    y, core = row // 2, row % 2
    z, x = col // NX, col % NX
    slots = values.shape[0]
    col_blocks = nodes.shape[0]
    count = count_ref[0, 0]
    start = Copies(send, recv)

    def ring(step):
        return lax.rem(y + step + NY, NY) * 2 + core

    def zof(dz):
        return lax.rem(z + dz + NZ, NZ)

    def xof(dx):
        return lax.rem(x + dx + NX, NX)

    def at(dz, dx):
        return (row, zof(dz) * NX + xof(dx))

    twin = (y * 2 + 1 - core, col)
    peers = [(ring(s), col) for s in (1, -1, 2, -2)] + [twin]
    peers += [at(s, 0) for s in (1, -1, 2, -2)] + [at(0, s) for s in (1, -1, 2)]
    barrier = pltpu.get_barrier_semaphore()
    for peer in peers:
        pl.semaphore_signal(barrier, inc=1, device_id=peer, device_id_type=MESH)
    load = pltpu.make_async_copy(values_hbm, values, local.at[0])
    load.start()
    keep = pltpu.make_async_copy(x_ref, slab.at[row], local.at[1])
    keep.start()
    pl.semaphore_wait(barrier, len(peers))

    middle = x_ref.shape[1] // 2

    def chunk(step, half=None):
        ref = slab.at[ring(step)]
        return ref if half is None else ref.at[:, half * middle : (half + 1) * middle]

    def forward(step, half, to):
        ref = chunk(step, half)
        return start(ref, ref, to)

    direct = {s: start(x_ref, slab.at[row], (ring(s), col)) for s in (2, -2, 1, -1)}
    twins = [start(x_ref, slab.at[row], twin)]

    for q in range(slots // LANES):
        lanes = jnp.broadcast_to(rows_ref[:, q * LANES : (q + 1) * LANES] // col_blocks, (LANES, LANES))
        spread[q * LANES : (q + 1) * LANES] = lanes.T
    earlier = lax.broadcasted_iota(i32, (slots, LANES), 0)
    lane = lax.broadcasted_iota(i32, (slots, LANES), 1)
    live = jnp.where(earlier < count, earlier + 1, 0)
    for q in range(slots // LANES):
        same = spread[...] == rows_ref[:, q * LANES : (q + 1) * LANES] // col_blocks
        ahead = earlier < lane + q * LANES
        index[q : q + 1] = jnp.max(jnp.where(same & ahead, live, 0), axis=0, keepdims=True)
    index[3:4] = jnp.max(jnp.where(spread[...] == lane, live, 0), axis=0, keepdims=True)
    fetch = pltpu.make_async_copy(index, index_smem, local.at[2])
    fetch.start()
    chain[0] = jnp.zeros(chain.shape[1:], f32)

    forwarded = {}
    for s in (1, -1):
        direct[s].wait_recv()
        twins.append(forward(-s, None, twin))

    def relayout(group, _):
        for t in range(HALF):
            rows = values[pl.ds(pl.multiple_of(group * 16, 16), 16), t * LANES : (t + 1) * LANES]
            flat[t * 17 : t * 17 + 16, :] = rows.astype(f32)
        for s in range(16):
            rows = flat[pl.ds(s, HALF, stride=17), :]
            blocks[group * 16 + s, 0:HALF] = rows.astype(b16)
            blocks[group * 16 + s, HALF:BLK] = pltpu.roll(rows, BLK, 1).astype(b16)
        return 0

    load.wait()
    groups = slots // 16
    lax.fori_loop(0, groups // 3, relayout, 0)
    for s in (2, -2):
        half = 0 if s > 0 else 1
        direct[s].wait_recv()
        forwarded[s // 2] = forward(-s, None, (ring(s // 2), col))
        forwarded[s] = forward(-s, half, (ring(s), col))
        twins.append(forward(-s, None, twin))
    lax.fori_loop(groups // 3, groups, relayout, 0)
    for s in (1, -1):
        forwarded[s].wait_recv()
        twins.append(forward(-3 * s, None, twin))
    for s in (2, -2):
        forwarded[s].wait_recv()
        twins.append(forward(4, 0 if s > 0 else 1, twin))
    keep.wait()
    fetch.wait()
    for copy in twins:
        copy.wait_recv()

    for j in range(x_ref.shape[1] // LANES):
        taken = slab[:, :, j * LANES : (j + 1) * LANES].astype(f32).reshape(LANES, LANES).T.astype(b16)
        for h in range(2):
            nodes[2 * j + h] = taken[h * BLK : (h + 1) * BLK]

    def product(slot):
        rows = nodes[lax.rem(codes_ref[0, slot], col_blocks)]
        return jnp.dot(blocks[slot, :, 0:BLK], rows, preferred_element_type=f32)

    def multiply(group, _):
        products = [product(group * UNROLL + u) for u in range(UNROLL)]
        for u in range(UNROLL):
            slot = group * UNROLL + u
            chain[slot + 1] = products[u] + chain[index_smem[slot // LANES, lax.rem(slot, LANES)]]
        return 0

    lax.fori_loop(0, slots // UNROLL, multiply, 0)

    def own(zz, xx, piece):
        block = index_smem[3, (zz * NX + xx) * OWNED + piece // 2]
        return chain[block, (piece % 2) * HALF : (piece % 2 + 1) * HALF]

    def wide(ref):
        return ref[...].astype(f32)

    ring_z, first = {}, {}

    def send_ring(step):
        for d in range(2):
            sign = 1 - 2 * d
            if step == 1:
                for xx in range(NX):
                    ring_out[d, 0, d, xx] = own(zof(4), xx, d).astype(b16)
                ring_z[4, d] = start(ring_out.at[d, 0, d], ring_in.at[d, 0, d], at(2 * sign, 0))
            for dz in (3, 1) if step == 1 else (2,):
                if dz == 2:
                    ring_z[4, d].wait_recv()
                    ring_z[3, d].wait_recv()
                for xx in range(NX):
                    for piece in range(2):
                        mine = own(zof(sign * dz), xx, piece)
                        if dz == 2:
                            mine = mine + wide(ring_in.at[d, 3, piece, xx])
                            if piece == d:
                                mine = mine + wide(ring_in.at[d, 0, piece, xx])
                        ring_out[d, dz, piece, xx] = mine.astype(b16)
                to = at(sign * (dz if dz < 3 else 1), 0)
                ring_z[dz, d] = start(ring_out.at[d, dz], ring_in.at[d, dz], to)

    def send_across(_):
        for d in range(2):
            ring_z[1, d].wait_recv()
            ring_z[2, d].wait_recv()
        for dx in (2, 1, -1, 0):
            for piece in range(2):
                value = own(z, xof(dx), piece)
                for d in range(2):
                    value = value + wide(ring_in.at[d, 1, piece, xof(dx)]) + wide(ring_in.at[d, 2, piece, xof(dx)])
                if dx == 0:
                    total[piece] = value
                else:
                    across_out[dx + 1, piece] = value.astype(b16)
            if dx != 0:
                first[dx] = start(across_out.at[dx + 1], across_in.at[dx + 1], at(0, dx))

    far, near, sums, straight, passed = {}, {}, {}, {}, {}
    places = [sum(len(group) for group in GROUPS[:g]) for g in range(len(GROUPS) + 1)]

    def along_x(out, into, d, g):
        span = pl.ds(places[g], len(GROUPS[g]))
        return start(out.at[d, span], into.at[d, span], at(0, 1 - 2 * d))

    def send_far(g):
        for d in range(2):
            for i, dz in enumerate(GROUPS[g], places[g]):
                for k in range(3):
                    far_out[d, i, k] = own(zof(dz), xof(2), 2 + 3 * d + k).astype(b16)
            far[g, d] = along_x(far_out, far_in, d, g)

    def send_near(g):
        for d in range(2):
            for i, dz in enumerate(GROUPS[g], places[g]):
                for k in range(3):
                    near_out[d, i, k] = own(zof(dz), xof(1 - 2 * d), 5 - 3 * d + k).astype(b16)
            near[g, d] = along_x(near_out, near_in, d, g)

    def send_sum(g):
        for d in range(2):
            far[g, d].wait_recv()
            for i, dz in enumerate(GROUPS[g], places[g]):
                for k in range(3):
                    mine = own(zof(dz), xof(1 - 2 * d), 2 + 3 * d + k)
                    sum_out[d, i, k] = (mine + wide(far_in.at[d, i, k])).astype(b16)
            sums[g, d] = along_x(sum_out, sum_in, d, g)

    def send_straight(g):
        for d in range(2):
            near[g, d].wait_recv()
            sums[g, d].wait_recv()
        for i, dz in enumerate(GROUPS[g], places[g]):
            if abs(dz) == 2:
                passed[2 * dz].wait_recv()
                passed[dz + dz // 2].wait_recv()
            for d in range(2):
                for k in range(3):
                    value = own(zof(dz), x, 2 + 3 * d + k)
                    value = value + (wide(sum_in.at[d, i, k]) + wide(near_in.at[1 - d, i, k]))
                    if abs(dz) == 2:
                        value = value + wide(straight_in.at[dz + dz // 2 + 3, d, k])
                    if dz == 2 - 4 * d:
                        value = value + wide(straight_in.at[7, d, k])
                    if dz == 0:
                        total[2 + 3 * d + k] = value
                    else:
                        straight_out[dz + 3, d, k] = value.astype(b16)
            src, dst = straight_out.at[dz + 3], straight_in.at[dz + 3]
            if dz == 4:
                for d in range(2):
                    passed[4 - 8 * d] = start(src.at[d], dst.at[d], at(2 - 4 * d, 0))
            elif abs(dz) == 3:
                passed[dz] = start(src, dst, at(dz // 3, 0))
            elif dz != 0:
                straight[dz] = start(src, dst, at(dz, 0))

    steps = {"A": send_ring, "X": send_across, "F": send_far, "N": send_near, "S": send_sum, "E": send_straight}
    for step in ORDER:
        steps[step[0]](int(step[1]))
    for dz, copy in straight.items():
        copy.wait_recv()
        for d in range(2):
            for k in range(3):
                total[2 + 3 * d + k] += wide(straight_in.at[dz + 3, d, k])
    for dx, copy in first.items():
        copy.wait_recv()
        for piece in range(2):
            total[piece] += wide(across_in.at[dx + 1, piece])

    for rb in range(OWNED):
        for h in range(2):
            mixed[pl.ds(rb * BLK + h, HALF, stride=2), :] = total[2 * rb + h]
    out_ref[...] = mixed[...].astype(b16)
    for copy in start.started:
        copy.wait_send()


def aggregate(codes, count, features_t, values):
    slots = codes.shape[1]
    rows, nodes = features_t.shape
    width = 2 * NY * rows
    vmem = pltpu.VMEM
    crossing = vmem((2, NZ, 3, HALF, width), b16)
    ring = vmem((2, 4, 2, NX, HALF, width), b16)
    across = vmem((NX, 2, HALF, width), b16)
    straight = vmem((NZ, 2, 3, HALF, width), b16)
    copies = 4 + 1 + 4 + 8 + 8 + NX - 1 + 6 * len(GROUPS) + NZ
    return pl.pallas_call(
        kernel,
        out_shape=jax.ShapeDtypeStruct((OWNED * BLK, width), b16),
        in_specs=[
            pl.BlockSpec(memory_space=pltpu.SMEM),
            pl.BlockSpec(memory_space=pltpu.VMEM),
            pl.BlockSpec(memory_space=pltpu.SMEM),
            pl.BlockSpec(memory_space=pl.ANY),
            pl.BlockSpec(memory_space=pl.ANY),
        ],
        out_specs=pl.BlockSpec(memory_space=pltpu.VMEM),
        scratch_shapes=[
            vmem((2 * NY, rows, nodes), b16),
            vmem((slots, BLK * BLK), b16),
            vmem((HALF * 17, LANES), f32),
            vmem((slots, BLK, LANES), b16),
            vmem((nodes // BLK, BLK, width), b16),
            vmem((slots, LANES), i32),
            vmem((8, LANES), i32),
            pltpu.SMEM((8, LANES), i32),
            vmem((slots + 1, BLK, width), f32),
        ]
        + [ring] * 2
        + [across] * 2
        + [crossing] * 6
        + [straight] * 2
        + [
            vmem((2 * OWNED, HALF, width), f32),
            vmem((OWNED * BLK, width), f32),
            pltpu.SemaphoreType.DMA((3,)),
            pltpu.SemaphoreType.DMA((copies,)),
            pltpu.SemaphoreType.DMA((copies,)),
        ],
        compiler_params=pltpu.CompilerParams(collective_id=0, has_side_effects=True, vmem_limit_bytes=VMEM_LIMIT),
    )(codes, codes, count, features_t, values)


def shards(features, block_codes, block_count, block_values, weight, bias):
    aggregated = aggregate(block_codes, block_count, features.T, block_values[0])
    hidden = jnp.dot(aggregated, weight, preferred_element_type=f32) + bias
    return jnp.maximum(hidden, 0.0).astype(b16)


def solution(mesh):
    in_specs = (P("col", "row"), P("row", "col"), P("row", "col"), P("row", "col", None), P(), P())
    out_specs = P(("row", "col"), None)
    return jax.shard_map(shards, mesh=mesh, in_specs=in_specs, out_specs=out_specs, check_vma=False)
```

```python
import jax
import jax.numpy as jnp
from jax import lax
from jax.experimental import pallas as pl
from jax.experimental.pallas import tpu as pltpu
from jax.sharding import PartitionSpec as P

BLK = 64
HALF = BLK // 2
LANES = 128
OWNED = 4
NX, NZ, NY = 4, 8, 8
UNROLL = 96
GROUPS = ((4,), (3, -3), (2, -2), (1, -1), (0,))
ORDER = ("F0", "F1", "A1", "F2", "F3", "F4", "S0", "N0", "S1", "A2", "N1", "E0", "S2", "N2")
ORDER += ("E1", "S3", "N3", "X0", "E2", "S4", "N4", "E3", "E4")
MESH = pl.DeviceIdType.MESH
VMEM_LIMIT = 56 << 20
f32, b16, i32 = jnp.float32, jnp.bfloat16, jnp.int32


class Copies:
    def __init__(self, send, recv):
        self.send, self.recv, self.started = send, recv, []

    def __call__(self, src, dst, to):
        slot = len(self.started)
        copy = pltpu.make_async_remote_copy(
            src_ref=src,
            dst_ref=dst,
            send_sem=self.send.at[slot],
            recv_sem=self.recv.at[slot],
            device_id=to,
            device_id_type=MESH,
        )
        copy.start()
        self.started.append(copy)
        return copy


def kernel(
    codes_ref, rows_ref, count_ref, x_ref, values_hbm, out_ref,
    slab, values, flat, blocks, nodes, spread, index, index_smem, chain,
    ring_out, ring_in, across_out, across_in, far_out, far_in, near_out, near_in, sum_out, sum_in,
    straight_out, straight_in, total, mixed,
    local, send, recv,
):
    row, col = lax.axis_index("row"), lax.axis_index("col")
    y, core = row // 2, row % 2
    z, x = col // NX, col % NX
    slots = values.shape[0]
    col_blocks = nodes.shape[0]
    count = count_ref[0, 0]
    start = Copies(send, recv)

    def ring(step):
        return lax.rem(y + step + NY, NY) * 2 + core

    def zof(dz):
        return lax.rem(z + dz + NZ, NZ)

    def xof(dx):
        return lax.rem(x + dx + NX, NX)

    def at(dz, dx):
        return (row, zof(dz) * NX + xof(dx))

    twin = (y * 2 + 1 - core, col)
    peers = [(ring(s), col) for s in (1, -1, 2, -2)] + [twin]
    peers += [at(s, 0) for s in (1, -1, 2, -2)] + [at(0, s) for s in (1, -1, 2)]
    barrier = pltpu.get_barrier_semaphore()
    for peer in peers:
        pl.semaphore_signal(barrier, inc=1, device_id=peer, device_id_type=MESH)
    load = pltpu.make_async_copy(values_hbm, values, local.at[0])
    load.start()
    keep = pltpu.make_async_copy(x_ref, slab.at[row], local.at[1])
    keep.start()
    pl.semaphore_wait(barrier, len(peers))

    middle = x_ref.shape[1] // 2

    def chunk(step, half=None):
        ref = slab.at[ring(step)]
        return ref if half is None else ref.at[:, half * middle : (half + 1) * middle]

    def forward(step, half, to):
        ref = chunk(step, half)
        return start(ref, ref, to)

    direct, whole = {}, slab.at[row]
    for s in (2, -2):
        for half in (0, 1) if s > 0 else (1, 0):
            span = pl.ds(half * middle, middle)
            direct[s, half] = start(x_ref.at[:, span], whole.at[:, span], (ring(s), col))
    for s in (1, -1):
        direct[s] = start(x_ref, whole, (ring(s), col))
    twins = [start(x_ref, slab.at[row], twin)]

    for q in range(slots // LANES):
        lanes = jnp.broadcast_to(rows_ref[:, q * LANES : (q + 1) * LANES] // col_blocks, (LANES, LANES))
        spread[q * LANES : (q + 1) * LANES] = lanes.T
    earlier = lax.broadcasted_iota(i32, (slots, LANES), 0)
    lane = lax.broadcasted_iota(i32, (slots, LANES), 1)
    live = jnp.where(earlier < count, earlier + 1, 0)
    for q in range(slots // LANES):
        same = spread[...] == rows_ref[:, q * LANES : (q + 1) * LANES] // col_blocks
        ahead = earlier < lane + q * LANES
        index[q : q + 1] = jnp.max(jnp.where(same & ahead, live, 0), axis=0, keepdims=True)
    index[3:4] = jnp.max(jnp.where(spread[...] == lane, live, 0), axis=0, keepdims=True)
    fetch = pltpu.make_async_copy(index, index_smem, local.at[2])
    fetch.start()
    chain[0] = jnp.zeros(chain.shape[1:], f32)

    forwarded = {}
    def relayout(group, _):
        for t in range(HALF):
            rows = values[pl.ds(pl.multiple_of(group * 16, 16), 16), t * LANES : (t + 1) * LANES]
            flat[t * 17 : t * 17 + 16, :] = rows.astype(f32)
        for s in range(16):
            rows = flat[pl.ds(s, HALF, stride=17), :]
            blocks[group * 16 + s, 0:HALF] = rows.astype(b16)
            blocks[group * 16 + s, HALF:BLK] = pltpu.roll(rows, BLK, 1).astype(b16)
        return 0

    load.wait()
    groups = slots // 16
    lax.fori_loop(0, groups // 6, relayout, 0)
    for s in (2, -2):
        half = 0 if s > 0 else 1
        direct[s, half].wait_recv()
        forwarded[s] = forward(-s, half, (ring(s), col))
        forwarded[s // 2, half] = forward(-s, half, (ring(s // 2), col))
    for s in (2, -2):
        half = 1 if s > 0 else 0
        direct[s, half].wait_recv()
        forwarded[s // 2, half] = forward(-s, half, (ring(s // 2), col))
        twins.append(forward(-s, None, twin))
    for s in (1, -1):
        direct[s].wait_recv()
        twins.append(forward(-s, None, twin))
    lax.fori_loop(groups // 6, groups, relayout, 0)
    for s in (1, -1):
        for half in range(2):
            forwarded[s, half].wait_recv()
        twins.append(forward(-3 * s, None, twin))
    for s in (2, -2):
        forwarded[s].wait_recv()
        twins.append(forward(4, 0 if s > 0 else 1, twin))
    keep.wait()
    fetch.wait()
    for copy in twins:
        copy.wait_recv()

    for j in range(x_ref.shape[1] // LANES):
        taken = slab[:, :, j * LANES : (j + 1) * LANES].astype(f32).reshape(LANES, LANES).T.astype(b16)
        for h in range(2):
            nodes[2 * j + h] = taken[h * BLK : (h + 1) * BLK]

    def product(slot):
        rows = nodes[lax.rem(codes_ref[0, slot], col_blocks)]
        return jnp.dot(blocks[slot, :, 0:BLK], rows, preferred_element_type=f32)

    def multiply(group, _):
        products = [product(group * UNROLL + u) for u in range(UNROLL)]
        for u in range(UNROLL):
            slot = group * UNROLL + u
            chain[slot + 1] = products[u] + chain[index_smem[slot // LANES, lax.rem(slot, LANES)]]
        return 0

    lax.fori_loop(0, slots // UNROLL, multiply, 0)

    def own(zz, xx, piece):
        block = index_smem[3, (zz * NX + xx) * OWNED + piece // 2]
        return chain[block, (piece % 2) * HALF : (piece % 2 + 1) * HALF]

    def wide(ref):
        return ref[...].astype(f32)

    ring_z, first = {}, {}

    def send_ring(step):
        for d in range(2):
            sign = 1 - 2 * d
            if step == 1:
                for xx in range(NX):
                    ring_out[d, 0, d, xx] = own(zof(4), xx, d).astype(b16)
                ring_z[4, d] = start(ring_out.at[d, 0, d], ring_in.at[d, 0, d], at(2 * sign, 0))
            for dz in (3, 1) if step == 1 else (2,):
                if dz == 2:
                    ring_z[4, d].wait_recv()
                    ring_z[3, d].wait_recv()
                for xx in range(NX):
                    for piece in range(2):
                        mine = own(zof(sign * dz), xx, piece)
                        if dz == 2:
                            mine = mine + wide(ring_in.at[d, 3, piece, xx])
                            if piece == d:
                                mine = mine + wide(ring_in.at[d, 0, piece, xx])
                        ring_out[d, dz, piece, xx] = mine.astype(b16)
                to = at(sign * (dz if dz < 3 else 1), 0)
                ring_z[dz, d] = start(ring_out.at[d, dz], ring_in.at[d, dz], to)

    def send_across(_):
        for d in range(2):
            ring_z[1, d].wait_recv()
            ring_z[2, d].wait_recv()
        for dx in (2, 1, -1, 0):
            for piece in range(2):
                value = own(z, xof(dx), piece)
                for d in range(2):
                    value = value + wide(ring_in.at[d, 1, piece, xof(dx)]) + wide(ring_in.at[d, 2, piece, xof(dx)])
                if dx == 0:
                    total[piece] = value
                else:
                    across_out[dx + 1, piece] = value.astype(b16)
            if dx != 0:
                first[dx] = start(across_out.at[dx + 1], across_in.at[dx + 1], at(0, dx))

    far, near, sums, straight, passed = {}, {}, {}, {}, {}
    places = [sum(len(group) for group in GROUPS[:g]) for g in range(len(GROUPS) + 1)]

    def along_x(out, into, d, g):
        span = pl.ds(places[g], len(GROUPS[g]))
        return start(out.at[d, span], into.at[d, span], at(0, 1 - 2 * d))

    def send_far(g):
        for d in range(2):
            for i, dz in enumerate(GROUPS[g], places[g]):
                for k in range(3):
                    far_out[d, i, k] = own(zof(dz), xof(2), 2 + 3 * d + k).astype(b16)
            far[g, d] = along_x(far_out, far_in, d, g)

    def send_near(g):
        for d in range(2):
            for i, dz in enumerate(GROUPS[g], places[g]):
                for k in range(3):
                    near_out[d, i, k] = own(zof(dz), xof(1 - 2 * d), 5 - 3 * d + k).astype(b16)
            near[g, d] = along_x(near_out, near_in, d, g)

    def send_sum(g):
        for d in range(2):
            far[g, d].wait_recv()
            for i, dz in enumerate(GROUPS[g], places[g]):
                for k in range(3):
                    mine = own(zof(dz), xof(1 - 2 * d), 2 + 3 * d + k)
                    sum_out[d, i, k] = (mine + wide(far_in.at[d, i, k])).astype(b16)
            sums[g, d] = along_x(sum_out, sum_in, d, g)

    def send_straight(g):
        for d in range(2):
            near[g, d].wait_recv()
            sums[g, d].wait_recv()
        for i, dz in enumerate(GROUPS[g], places[g]):
            if abs(dz) == 2:
                passed[2 * dz].wait_recv()
                passed[dz + dz // 2].wait_recv()
            for d in range(2):
                for k in range(3):
                    value = own(zof(dz), x, 2 + 3 * d + k)
                    value = value + (wide(sum_in.at[d, i, k]) + wide(near_in.at[1 - d, i, k]))
                    if abs(dz) == 2:
                        value = value + wide(straight_in.at[dz + dz // 2 + 3, d, k])
                    if dz == 2 - 4 * d:
                        value = value + wide(straight_in.at[7, d, k])
                    if dz == 0:
                        total[2 + 3 * d + k] = value
                    else:
                        straight_out[dz + 3, d, k] = value.astype(b16)
            src, dst = straight_out.at[dz + 3], straight_in.at[dz + 3]
            if dz == 4:
                for d in range(2):
                    passed[4 - 8 * d] = start(src.at[d], dst.at[d], at(2 - 4 * d, 0))
            elif abs(dz) == 3:
                passed[dz] = start(src, dst, at(dz // 3, 0))
            elif dz != 0:
                straight[dz] = start(src, dst, at(dz, 0))

    steps = {"A": send_ring, "X": send_across, "F": send_far, "N": send_near, "S": send_sum, "E": send_straight}
    for step in ORDER:
        steps[step[0]](int(step[1]))
    for dz, copy in straight.items():
        copy.wait_recv()
        for d in range(2):
            for k in range(3):
                total[2 + 3 * d + k] += wide(straight_in.at[dz + 3, d, k])
    for dx, copy in first.items():
        copy.wait_recv()
        for piece in range(2):
            total[piece] += wide(across_in.at[dx + 1, piece])

    for rb in range(OWNED):
        for h in range(2):
            mixed[pl.ds(rb * BLK + h, HALF, stride=2), :] = total[2 * rb + h]
    out_ref[...] = mixed[...].astype(b16)
    for copy in start.started:
        copy.wait_send()


def aggregate(codes, count, features_t, values):
    slots = codes.shape[1]
    rows, nodes = features_t.shape
    width = 2 * NY * rows
    vmem = pltpu.VMEM
    crossing = vmem((2, NZ, 3, HALF, width), b16)
    ring = vmem((2, 4, 2, NX, HALF, width), b16)
    across = vmem((NX, 2, HALF, width), b16)
    straight = vmem((NZ, 2, 3, HALF, width), b16)
    copies = 4 + 4 + 1 + 4 + 8 + 8 + NX - 1 + 6 * len(GROUPS) + NZ
    return pl.pallas_call(
        kernel,
        out_shape=jax.ShapeDtypeStruct((OWNED * BLK, width), b16),
        in_specs=[
            pl.BlockSpec(memory_space=pltpu.SMEM),
            pl.BlockSpec(memory_space=pltpu.VMEM),
            pl.BlockSpec(memory_space=pltpu.SMEM),
            pl.BlockSpec(memory_space=pl.ANY),
            pl.BlockSpec(memory_space=pl.ANY),
        ],
        out_specs=pl.BlockSpec(memory_space=pltpu.VMEM),
        scratch_shapes=[
            vmem((2 * NY, rows, nodes), b16),
            vmem((slots, BLK * BLK), b16),
            vmem((HALF * 17, LANES), f32),
            vmem((slots, BLK, LANES), b16),
            vmem((nodes // BLK, BLK, width), b16),
            vmem((slots, LANES), i32),
            vmem((8, LANES), i32),
            pltpu.SMEM((8, LANES), i32),
            vmem((slots + 1, BLK, width), f32),
        ]
        + [ring] * 2
        + [across] * 2
        + [crossing] * 6
        + [straight] * 2
        + [
            vmem((2 * OWNED, HALF, width), f32),
            vmem((OWNED * BLK, width), f32),
            pltpu.SemaphoreType.DMA((3,)),
            pltpu.SemaphoreType.DMA((copies,)),
            pltpu.SemaphoreType.DMA((copies,)),
        ],
        compiler_params=pltpu.CompilerParams(collective_id=0, has_side_effects=True, vmem_limit_bytes=VMEM_LIMIT),
    )(codes, codes, count, features_t, values)


def shards(features, block_codes, block_count, block_values, weight, bias):
    aggregated = aggregate(block_codes, block_count, features.T, block_values[0])
    hidden = jnp.dot(aggregated, weight, preferred_element_type=f32) + bias
    return jnp.maximum(hidden, 0.0).astype(b16)


def solution(mesh):
    in_specs = (P("col", "row"), P("row", "col"), P("row", "col"), P("row", "col", None), P(), P())
    out_specs = P(("row", "col"), None)
    return jax.shard_map(shards, mesh=mesh, in_specs=in_specs, out_specs=out_specs, check_vma=False)
```

```python
import jax
import jax.numpy as jnp
from jax import lax
from jax.experimental import pallas as pl
from jax.experimental.pallas import tpu as pltpu
from jax.sharding import PartitionSpec as P

BLK = 64
HALF = BLK // 2
LANES = 128
OWNED = 4
NX, NZ, NY = 4, 8, 8
UNROLL = 96
GROUPS = ((4,), (3, -3), (2, -2), (1, -1), (0,))
ORDER = ("F0", "F1", "A1", "F2", "F3", "F4", "S0", "N0", "S1", "A2", "N1", "E0", "S2", "N2")
ORDER += ("E1", "S3", "N3", "X0", "E2", "S4", "N4", "E3", "E4")
MESH = pl.DeviceIdType.MESH
VMEM_LIMIT = 56 << 20
f32, b16, i32 = jnp.float32, jnp.bfloat16, jnp.int32


class Copies:
    def __init__(self, send, recv):
        self.send, self.recv, self.started = send, recv, []

    def __call__(self, src, dst, to):
        slot = len(self.started)
        copy = pltpu.make_async_remote_copy(
            src_ref=src,
            dst_ref=dst,
            send_sem=self.send.at[slot],
            recv_sem=self.recv.at[slot],
            device_id=to,
            device_id_type=MESH,
        )
        copy.start()
        self.started.append(copy)
        return copy


def kernel(
    codes_hbm, count_ref, x_ref, values_hbm, out_ref,
    codes_ref, rows_ref, slab, values, flat, blocks, nodes, spread, index, index_smem, chain,
    ring_out, ring_in, across_out, across_in, far_out, far_in, near_out, near_in, sum_out, sum_in,
    straight_out, straight_in, total, mixed,
    local, send, recv,
):
    row, col = lax.axis_index("row"), lax.axis_index("col")
    y, core = row // 2, row % 2
    z, x = col // NX, col % NX
    slots = values.shape[0]
    col_blocks = nodes.shape[0]
    start = Copies(send, recv)

    def ring(step):
        return lax.rem(y + step + NY, NY) * 2 + core

    def zof(dz):
        return lax.rem(z + dz + NZ, NZ)

    def xof(dx):
        return lax.rem(x + dx + NX, NX)

    def at(dz, dx):
        return (row, zof(dz) * NX + xof(dx))

    twin = (y * 2 + 1 - core, col)
    peers = [(ring(s), col) for s in (1, -1, 2, -2)] + [twin]
    peers += [at(s, 0) for s in (1, -1, 2, -2)] + [at(0, s) for s in (1, -1, 2)]
    barrier = pltpu.get_barrier_semaphore()
    for peer in peers:
        pl.semaphore_signal(barrier, inc=1, device_id=peer, device_id_type=MESH)
    small = [pltpu.make_async_copy(codes_hbm, ref, local.at[3 + i]) for i, ref in enumerate((rows_ref, codes_ref))]
    for copy in small:
        copy.start()
    load = pltpu.make_async_copy(values_hbm, values, local.at[0])
    load.start()
    keep = pltpu.make_async_copy(x_ref, slab.at[row], local.at[1])
    keep.start()
    pl.semaphore_wait(barrier, len(peers))

    middle = x_ref.shape[1] // 2

    def chunk(step, half=None):
        ref = slab.at[ring(step)]
        return ref if half is None else ref.at[:, half * middle : (half + 1) * middle]

    def forward(step, half, to):
        ref = chunk(step, half)
        return start(ref, ref, to)

    direct, whole = {}, slab.at[row]
    for s in (2, -2):
        for half in (0, 1) if s > 0 else (1, 0):
            span = pl.ds(half * middle, middle)
            direct[s, half] = start(x_ref.at[:, span], whole.at[:, span], (ring(s), col))
    for s in (1, -1):
        direct[s] = start(x_ref, whole, (ring(s), col))
    twins = [start(x_ref, slab.at[row], twin)]

    for copy in small:
        copy.wait()
    for q in range(slots // LANES):
        lanes = jnp.broadcast_to(rows_ref[:, q * LANES : (q + 1) * LANES] // col_blocks, (LANES, LANES))
        spread[q * LANES : (q + 1) * LANES] = lanes.T
    earlier = lax.broadcasted_iota(i32, (slots, LANES), 0)
    lane = lax.broadcasted_iota(i32, (slots, LANES), 1)
    live = jnp.where(earlier < count_ref[0, 0], earlier + 1, 0)
    for q in range(slots // LANES):
        same = spread[...] == rows_ref[:, q * LANES : (q + 1) * LANES] // col_blocks
        ahead = earlier < lane + q * LANES
        index[q : q + 1] = jnp.max(jnp.where(same & ahead, live, 0), axis=0, keepdims=True)
    index[3:4] = jnp.max(jnp.where(spread[...] == lane, live, 0), axis=0, keepdims=True)
    fetch = pltpu.make_async_copy(index, index_smem, local.at[2])
    fetch.start()
    chain[0] = jnp.zeros(chain.shape[1:], f32)

    forwarded = {}
    def relayout(group, _):
        for t in range(HALF):
            rows = values[pl.ds(pl.multiple_of(group * 16, 16), 16), t * LANES : (t + 1) * LANES]
            flat[t * 17 : t * 17 + 16, :] = rows.astype(f32)
        for s in range(16):
            rows = flat[pl.ds(s, HALF, stride=17), :]
            blocks[group * 16 + s, 0:HALF] = rows.astype(b16)
            blocks[group * 16 + s, HALF:BLK] = pltpu.roll(rows, BLK, 1).astype(b16)
        return 0

    load.wait()
    groups = slots // 16
    lax.fori_loop(0, groups // 6, relayout, 0)
    for s in (2, -2):
        half = 0 if s > 0 else 1
        direct[s, half].wait_recv()
        forwarded[s] = forward(-s, half, (ring(s), col))
        forwarded[s // 2, half] = forward(-s, half, (ring(s // 2), col))
    for s in (2, -2):
        half = 1 if s > 0 else 0
        direct[s, half].wait_recv()
        forwarded[s // 2, half] = forward(-s, half, (ring(s // 2), col))
        twins.append(forward(-s, None, twin))
    for s in (1, -1):
        direct[s].wait_recv()
        twins.append(forward(-s, None, twin))
    lax.fori_loop(groups // 6, groups, relayout, 0)
    for s in (1, -1):
        for half in range(2):
            forwarded[s, half].wait_recv()
        twins.append(forward(-3 * s, None, twin))
    for s in (2, -2):
        forwarded[s].wait_recv()
        twins.append(forward(4, 0 if s > 0 else 1, twin))
    keep.wait()
    fetch.wait()
    for copy in twins:
        copy.wait_recv()

    for j in range(x_ref.shape[1] // LANES):
        taken = slab[:, :, j * LANES : (j + 1) * LANES].astype(f32).reshape(LANES, LANES).T.astype(b16)
        for h in range(2):
            nodes[2 * j + h] = taken[h * BLK : (h + 1) * BLK]

    def product(slot):
        rows = nodes[lax.rem(codes_ref[0, slot], col_blocks)]
        return jnp.dot(blocks[slot, :, 0:BLK], rows, preferred_element_type=f32)

    def multiply(group, _):
        products = [product(group * UNROLL + u) for u in range(UNROLL)]
        for u in range(UNROLL):
            slot = group * UNROLL + u
            chain[slot + 1] = products[u] + chain[index_smem[slot // LANES, lax.rem(slot, LANES)]]
        return 0

    lax.fori_loop(0, slots // UNROLL, multiply, 0)

    def own(zz, xx, piece):
        block = index_smem[3, (zz * NX + xx) * OWNED + piece // 2]
        return chain[block, (piece % 2) * HALF : (piece % 2 + 1) * HALF]

    def wide(ref):
        return ref[...].astype(f32)

    ring_z, first = {}, {}

    def send_ring(step):
        for d in range(2):
            sign = 1 - 2 * d
            if step == 1:
                for xx in range(NX):
                    ring_out[d, 0, d, xx] = own(zof(4), xx, d).astype(b16)
                ring_z[4, d] = start(ring_out.at[d, 0, d], ring_in.at[d, 0, d], at(2 * sign, 0))
            for dz in (3, 1) if step == 1 else (2,):
                if dz == 2:
                    ring_z[4, d].wait_recv()
                    ring_z[3, d].wait_recv()
                for xx in range(NX):
                    for piece in range(2):
                        mine = own(zof(sign * dz), xx, piece)
                        if dz == 2:
                            mine = mine + wide(ring_in.at[d, 3, piece, xx])
                            if piece == d:
                                mine = mine + wide(ring_in.at[d, 0, piece, xx])
                        ring_out[d, dz, piece, xx] = mine.astype(b16)
                to = at(sign * (dz if dz < 3 else 1), 0)
                ring_z[dz, d] = start(ring_out.at[d, dz], ring_in.at[d, dz], to)

    def send_across(_):
        for d in range(2):
            ring_z[1, d].wait_recv()
            ring_z[2, d].wait_recv()
        for dx in (2, 1, -1, 0):
            for piece in range(2):
                value = own(z, xof(dx), piece)
                for d in range(2):
                    value = value + wide(ring_in.at[d, 1, piece, xof(dx)]) + wide(ring_in.at[d, 2, piece, xof(dx)])
                if dx == 0:
                    total[piece] = value
                else:
                    across_out[dx + 1, piece] = value.astype(b16)
            if dx != 0:
                first[dx] = start(across_out.at[dx + 1], across_in.at[dx + 1], at(0, dx))

    far, near, sums, straight, passed = {}, {}, {}, {}, {}
    places = [sum(len(group) for group in GROUPS[:g]) for g in range(len(GROUPS) + 1)]

    def along_x(out, into, d, g):
        span = pl.ds(places[g], len(GROUPS[g]))
        return start(out.at[d, span], into.at[d, span], at(0, 1 - 2 * d))

    def send_far(g):
        for d in range(2):
            for i, dz in enumerate(GROUPS[g], places[g]):
                for k in range(3):
                    far_out[d, i, k] = own(zof(dz), xof(2), 2 + 3 * d + k).astype(b16)
            far[g, d] = along_x(far_out, far_in, d, g)

    def send_near(g):
        for d in range(2):
            for i, dz in enumerate(GROUPS[g], places[g]):
                for k in range(3):
                    near_out[d, i, k] = own(zof(dz), xof(1 - 2 * d), 5 - 3 * d + k).astype(b16)
            near[g, d] = along_x(near_out, near_in, d, g)

    def send_sum(g):
        for d in range(2):
            far[g, d].wait_recv()
            for i, dz in enumerate(GROUPS[g], places[g]):
                for k in range(3):
                    mine = own(zof(dz), xof(1 - 2 * d), 2 + 3 * d + k)
                    sum_out[d, i, k] = (mine + wide(far_in.at[d, i, k])).astype(b16)
            sums[g, d] = along_x(sum_out, sum_in, d, g)

    def send_straight(g):
        for d in range(2):
            near[g, d].wait_recv()
            sums[g, d].wait_recv()
        for i, dz in enumerate(GROUPS[g], places[g]):
            if abs(dz) == 2:
                passed[2 * dz].wait_recv()
                passed[dz + dz // 2].wait_recv()
            for d in range(2):
                for k in range(3):
                    value = own(zof(dz), x, 2 + 3 * d + k)
                    value = value + (wide(sum_in.at[d, i, k]) + wide(near_in.at[1 - d, i, k]))
                    if abs(dz) == 2:
                        value = value + wide(straight_in.at[dz + dz // 2 + 3, d, k])
                    if dz == 2 - 4 * d:
                        value = value + wide(straight_in.at[7, d, k])
                    if dz == 0:
                        total[2 + 3 * d + k] = value
                    else:
                        straight_out[dz + 3, d, k] = value.astype(b16)
            src, dst = straight_out.at[dz + 3], straight_in.at[dz + 3]
            if dz == 4:
                for d in range(2):
                    passed[4 - 8 * d] = start(src.at[d], dst.at[d], at(2 - 4 * d, 0))
            elif abs(dz) == 3:
                passed[dz] = start(src, dst, at(dz // 3, 0))
            elif dz != 0:
                straight[dz] = start(src, dst, at(dz, 0))

    steps = {"A": send_ring, "X": send_across, "F": send_far, "N": send_near, "S": send_sum, "E": send_straight}
    for step in ORDER:
        steps[step[0]](int(step[1]))
    for dz, copy in straight.items():
        copy.wait_recv()
        for d in range(2):
            for k in range(3):
                total[2 + 3 * d + k] += wide(straight_in.at[dz + 3, d, k])
    for dx, copy in first.items():
        copy.wait_recv()
        for piece in range(2):
            total[piece] += wide(across_in.at[dx + 1, piece])

    for rb in range(OWNED):
        for h in range(2):
            mixed[pl.ds(rb * BLK + h, HALF, stride=2), :] = total[2 * rb + h]
    out_ref[...] = mixed[...].astype(b16)
    for copy in start.started:
        copy.wait_send()


def aggregate(codes, count, features_t, values):
    slots = codes.shape[1]
    rows, nodes = features_t.shape
    width = 2 * NY * rows
    vmem = pltpu.VMEM
    crossing = vmem((2, NZ, 3, HALF, width), b16)
    ring = vmem((2, 4, 2, NX, HALF, width), b16)
    across = vmem((NX, 2, HALF, width), b16)
    straight = vmem((NZ, 2, 3, HALF, width), b16)
    copies = 4 + 4 + 1 + 4 + 8 + 8 + NX - 1 + 6 * len(GROUPS) + NZ
    return pl.pallas_call(
        kernel,
        out_shape=jax.ShapeDtypeStruct((OWNED * BLK, width), b16),
        in_specs=[
            pl.BlockSpec(memory_space=pltpu.HBM),
            pl.BlockSpec(memory_space=pltpu.SMEM),
            pl.BlockSpec(memory_space=pltpu.HBM),
            pl.BlockSpec(memory_space=pltpu.HBM),
        ],
        out_specs=pl.BlockSpec(memory_space=pltpu.VMEM),
        scratch_shapes=[
            pltpu.SMEM(codes.shape, i32),
            vmem(codes.shape, i32),
            vmem((2 * NY, rows, nodes), b16),
            vmem((slots, BLK * BLK), b16),
            vmem((HALF * 17, LANES), f32),
            vmem((slots, BLK, LANES), b16),
            vmem((nodes // BLK, BLK, width), b16),
            vmem((slots, LANES), i32),
            vmem((8, LANES), i32),
            pltpu.SMEM((8, LANES), i32),
            vmem((slots + 1, BLK, width), f32),
        ]
        + [ring] * 2
        + [across] * 2
        + [crossing] * 6
        + [straight] * 2
        + [
            vmem((2 * OWNED, HALF, width), f32),
            vmem((OWNED * BLK, width), f32),
            pltpu.SemaphoreType.DMA((5,)),
            pltpu.SemaphoreType.DMA((copies,)),
            pltpu.SemaphoreType.DMA((copies,)),
        ],
        compiler_params=pltpu.CompilerParams(collective_id=0, has_side_effects=True, vmem_limit_bytes=VMEM_LIMIT),
    )(codes, count, features_t, values)


def shards(features, block_codes, block_count, block_values, weight, bias):
    aggregated = aggregate(block_codes, block_count, features.T, block_values[0])
    hidden = jnp.dot(aggregated, weight, preferred_element_type=f32) + bias
    return jnp.maximum(hidden, 0.0).astype(b16)


def solution(mesh):
    in_specs = (P("col", "row"), P("row", "col"), P("row", "col"), P("row", "col", None), P(), P())
    out_specs = P(("row", "col"), None)
    return jax.shard_map(shards, mesh=mesh, in_specs=in_specs, out_specs=out_specs, check_vma=False)
```
